512 devices in a mesh: wide: 64 (over z, y_hi, core), narrow: 8 (over y_lo, x).
Axes of the slice: x: 4, y: 8 (y_hi: 4, y_lo: 2; y = y_hi * 2 + y_lo), z: 8, core: 2. Of those that a mesh axis runs over, the one named last changes fastest.
Arguments:
- tile_values: bfloat16 [3584, 512, 512], P(('wide', 'narrow')), may hold values from -0.25 to 0.25
- tile_row: int32 [3584], P(('wide', 'narrow')), may hold values from 0 to 1
- tile_col: int32 [3584], P(('wide', 'narrow')), may hold values from 0 to 7
- basis: float32 [524288, 256], P(('wide', 'narrow')), may hold values from -6 to 6
Outputs:
- next_basis: float32 [4096, 256], P('wide')
The draws below stay inside these ranges and needn't reach their ends.
All inputs are finite; a program needn't handle non-finite values.
Results may differ from the reference program's by a relative error of at most 0.0032.
Values sent between devices are 32-bit elements; how exact they have to be, the bound alone decides.
No kernel may reach another device: no remote copies, remote signals or barrier semaphores. Data moves between devices by JAX's collectives and lax.ppermute only.
A program may use at most 64 MiB of HBM per device.

```python
import math
import jax
import jax.numpy as jnp
import numpy as np
from jax import lax

TILE = 512
RANK = 256
BLOCKS_DEV = 2
TILE_DEV = 7
COLS = 4096
COL_BLOCKS = 8
TILES = 3584
ROWS = 524288


def set_ends(result, own_key, least, largest):
    place = [jax.random.randint(jax.random.fold_in(own_key, axis), (), 0, length) for axis, length in enumerate(result.shape)]
    main_axis = result.shape.index(max(result.shape))
    neighbour = place[:main_axis] + [(place[main_axis] + 1) % result.shape[main_axis]] + place[main_axis + 1:]
    return result.at[tuple(place)].set(least).at[tuple(neighbour)].set(largest)


def steps_of(own_key, dims, shards, low, high):
    loudness, own = 1.0, jax.random.fold_in(own_key, 6)
    for axis_at, shards_of in shards:
        heights = jnp.exp(jax.random.uniform(jax.random.fold_in(own, axis_at), (shards_of,), jnp.float32, low / len(shards), high / len(shards)))
        loudness = loudness * jnp.repeat(heights, dims[axis_at] // shards_of).reshape([-1 if axis == axis_at else 1 for axis in range(len(dims))])
    return loudness


def cumulative_ranks(amount, slope):
    loads = [(1 << 20) // math.isqrt(standing ** slope) + 1 for standing in range(1, amount + 1)]
    width = 1 + sum(loads) // (1 << 30)
    return np.cumsum(np.array([max(1, weight // width) for weight in loads]))


def ranked_ids(own_key, shape, count, lean):
    listing = cumulative_ranks(count, lean)
    ticket = jax.random.randint(jax.random.fold_in(own_key, 1), shape, 0, int(listing[count - 1]))
    standing = jnp.searchsorted(jnp.asarray(listing, jnp.int32), ticket, side="right")
    return jax.random.permutation(jax.random.fold_in(own_key, 2), count)[standing].astype(jnp.int32)


def scatter_about(own_key, dims, width, bound, pieces=(), held_as=jnp.bfloat16):
    values = jax.random.normal(own_key, dims, jnp.float32) * width
    if len(pieces) > 0:
        values = steps_of(own_key, dims, pieces, -0.22, 0.18) * values
    return jnp.clip(values, min=-bound, max=bound).astype(held_as)


def setup_inputs(seed: int = 0) -> dict:
    key_of = jax.random.split(jax.random.key(seed), 5)
    return {
        "tile_values": scatter_about(key_of[0], (TILES, TILE, TILE), TILE ** -0.5, 0.25, ((0, 512),)),
        "tile_row": set_ends(jax.random.randint(key_of[1], (TILES,), 0, BLOCKS_DEV), jax.random.fold_in(key_of[1], 1), 0, BLOCKS_DEV - 1).astype(jnp.int32),
        "tile_col": set_ends(ranked_ids(key_of[2], (TILES,), COL_BLOCKS, 3), jax.random.fold_in(key_of[2], 3), 0, COL_BLOCKS - 1).astype(jnp.int32),
        "basis": scatter_about(key_of[3], (ROWS, RANK), 1.0, 6.0, ((0, 512),), jnp.float32),
    }


def reference(tile_values, tile_row, tile_col, basis):
    devices = TILES // TILE_DEV
    rounded = basis.astype(jnp.bfloat16)
    rounded = lax.optimization_barrier(rounded).astype(jnp.float32)
    rounded = rounded.reshape(devices, BLOCKS_DEV, TILE, RANK)
    tile_groups = tile_values.reshape(devices, TILE_DEV, TILE, TILE)
    row_groups = tile_row.reshape(devices, TILE_DEV)
    col_groups = tile_col.reshape(devices, TILE_DEV)

    def accumulate(running, inputs):
        group_tiles, group_rows, group_cols, blocks = inputs
        chosen = jnp.take(blocks, group_rows, axis=0)
        products = jnp.einsum('tij,tik->tjk', group_tiles.astype(jnp.float32), chosen, precision=lax.Precision.HIGHEST)
        one_hot = (group_cols[None, :] == jnp.arange(COL_BLOCKS, dtype=jnp.int32)[:, None]).astype(jnp.float32)
        return (running + jnp.einsum('ct,tjk->cjk', one_hot, products, precision=lax.Precision.HIGHEST), None)
    start = jnp.zeros((COL_BLOCKS, TILE, RANK), jnp.float32)
    summed, _ = lax.scan(accumulate, start, (tile_groups, row_groups, col_groups, rounded))
    gathered = summed.reshape(COLS, RANK)
    gram_sum = jnp.dot(gathered.T.astype(jnp.float32), gathered.astype(jnp.float32), precision=lax.Precision.HIGHEST, preferred_element_type=jnp.float32) / COLS
    factor = jnp.linalg.cholesky(gram_sum)
    return jax.scipy.linalg.solve_triangular(factor, gathered.T, lower=True).T
```

```python
import functools

import jax
import jax.numpy as jnp
from jax import lax
from jax.experimental import pallas as pl
from jax.experimental.pallas import tpu as pltpu
from jax.sharding import Mesh
from jax.sharding import PartitionSpec as P

AXES = ("z", "yh", "core", "yl", "x")
SIZES = (8, 4, 2, 2, 4)
TILE = 512
RANK = 256
COLS = 4096
HIGHEST = lax.Precision.HIGHEST
SUPER = 64


def product_kernel(row_ref, col_ref, core_ref, tile_ref, basis_ref, keep_ref, send_ref, rounded, total):
    step = pl.program_id(0)

    @pl.when(step == 0)
    def _():
        rounded[...] = basis_ref[...].astype(jnp.bfloat16).reshape(rounded.shape)
        total[...] = jnp.zeros_like(total)

    c = col_ref[step]
    res = lax.dot_general(
        tile_ref[0],
        rounded[row_ref[step]],
        (((0,), (0,)), ((), ())),
        preferred_element_type=jnp.float32,
    )
    for yh in range(4):
        for core in range(2):
            for yl in range(2):
                for x in range(4):
                    i = ((yh * 2 + core) * 2 + yl) * 4 + x
                    total[core, x, c, yh * 2 + yl] += res[8 * i : 8 * i + 8, :]

    @pl.when(step == pl.num_programs(0) - 1)
    def _():
        mine = core_ref[0]
        keep_ref[...] = total[mine]
        send_ref[...] = total[1 - mine]


def local_product(tile_values, tile_row, tile_col, basis, core):
    tiles = tile_values.shape[0]
    blocks = basis.shape[0] // TILE
    half = (4, 8, 8, 8, RANK)
    out = jax.ShapeDtypeStruct(half, jnp.float32)
    whole = pl.BlockSpec(half, lambda t, *_: (0, 0, 0, 0, 0))
    return pl.pallas_call(
        product_kernel,
        grid_spec=pltpu.PrefetchScalarGridSpec(
            num_scalar_prefetch=3,
            grid=(tiles,),
            in_specs=[
                pl.BlockSpec((1, TILE, TILE), lambda t, *_: (t, 0, 0)),
                pl.BlockSpec(basis.shape, lambda t, *_: (0, 0)),
            ],
            out_specs=[whole, whole],
            scratch_shapes=[
                pltpu.VMEM((blocks, TILE, RANK), jnp.bfloat16),
                pltpu.VMEM((2,) + half, jnp.float32),
            ],
        ),
        out_shape=[out, out],
        name="local_product",
    )(tile_row, tile_col, core, tile_values, basis)


def spread_kernel(parts_ref, out_ref):
    total = jnp.sum(parts_ref[...], axis=0)
    for i in range(out_ref.shape[0]):
        out_ref[i] = total


def sum_and_spread(parts, copies):
    return pl.pallas_call(
        spread_kernel,
        out_shape=jax.ShapeDtypeStruct((copies,) + parts.shape[1:], parts.dtype),
        name="sum_and_spread",
    )(parts)


def gram_kernel(rows_ref, out_ref):
    rows = rows_ref[...]
    gram = lax.dot_general(
        rows,
        rows,
        (((0,), (0,)), ((), ())),
        precision=HIGHEST,
        preferred_element_type=jnp.float32,
    )
    for i in range(RANK // 8):
        for h in range(2):
            out_ref[2 * i + h] = gram[8 * i : 8 * i + 8, 128 * h : 128 * h + 128]


def gram_terms(rows):
    return pl.pallas_call(
        gram_kernel,
        out_shape=jax.ShapeDtypeStruct((64, 8, 128), jnp.float32),
        name="gram_terms",
    )(rows)


def lane(v, j):
    return jnp.broadcast_to(v[:, j : j + 1], (8, 128))


def sub(v, i):
    return jnp.broadcast_to(v[i : i + 1, :], v.shape)


def invert_factor(block, at):
    e = {}
    for j in range(8):
        column = lane(block, at + j)
        for i in range(j, 8):
            e[i, j] = sub(column, i)
    inv = {}
    for j in range(8):
        p = e[j, j]
        r = lax.rsqrt(p)
        r = r * (1.5 - 0.5 * (p * r) * r)
        inv[j, j] = r
        for i in range(j + 1, 8):
            e[i, j] = e[i, j] * r
        for k in range(j + 1, 8):
            for i in range(k, 8):
                e[i, k] = e[i, k] - e[i, j] * e[k, j]
    for i in range(1, 8):
        for j in range(i):
            acc = e[i, j] * inv[j, j]
            for k in range(j + 1, i):
                acc = acc + e[i, k] * inv[k, j]
            inv[i, j] = -acc * inv[i, i]
    place = lax.broadcasted_iota(jnp.int32, (8, 128), 0)
    zero = jnp.zeros((8, 128), jnp.float32)
    lower, upper = [], []
    for j in range(8):
        down = zero
        for i in range(j, 8):
            down = jnp.where(place == i, inv[i, j], down)
        lower.append(down)
        across = zero
        for i in range(j + 1):
            across = jnp.where(place == i, inv[j, i], across)
        upper.append(across)
    return lower, upper


def combine(columns, rows):
    out = []
    for piece in rows:
        acc = columns[0] * sub(piece, 0)
        for j in range(1, 8):
            acc = acc + columns[j] * sub(piece, j)
        out.append(acc)
    return out


def finish_kernel(gram_ref, rows_ref, out_ref, s_ref, a_ref, u_ref, ua_ref, y_ref):
    for i in range(RANK // 8):
        for h in range(2):
            s_ref[8 * i : 8 * i + 8, 128 * h : 128 * h + 128] = gram_ref[2 * i + h] * (1.0 / COLS)
    rows = rows_ref[...]
    a_ref[...] = jnp.concatenate([rows, jnp.zeros_like(rows)], axis=0).T

    def group(g, carry):
        first = pl.multiple_of(g * SUPER, SUPER)
        u_ref[...] = s_ref[pl.ds(first, SUPER), :]
        ua_ref[...] = a_ref[pl.ds(first, SUPER), :]
        panels = SUPER // 8
        for k in range(panels):
            here = slice(8 * k, 8 * k + 8)
            pieces = [u_ref[here, 0:128], u_ref[here, 128:256], ua_ref[here, :]]
            lower, upper = invert_factor(pieces[0], 8 * k)
            scaled = combine(lower, pieces)
            u_ref[here, 0:128] = scaled[0]
            u_ref[here, 128:256] = scaled[1]
            ua_ref[here, :] = scaled[2]
            if k + 1 < panels:
                w = combine(upper, scaled)
                wide_rows = [[sub(piece, j) for j in range(8)] for piece in w]
                for q in range(k + 1, panels):
                    there = slice(8 * q, 8 * q + 8)
                    old = [u_ref[there, 0:128], u_ref[there, 128:256], ua_ref[there, :]]
                    ms = [lane(old[0], 8 * k + j) for j in range(8)]
                    new = []
                    for piece, wr in zip(old, wide_rows):
                        acc = piece
                        for j in range(8):
                            acc = acc - ms[j] * wr[j]
                        new.append(acc)
                    u_ref[there, 0:128] = new[0]
                    u_ref[there, 128:256] = new[1]
                    ua_ref[there, :] = new[2]
        u, ua = u_ref[...], ua_ref[...]
        y_ref[pl.ds(first, SUPER), :] = ua

        @pl.when(g + 1 < RANK // SUPER)
        def _():
            dims = (((0,), (0,)), ((), ()))
            left = u
            back = pltpu.roll(left, first, 1)
            s_new = s_ref[...] - lax.dot_general(back, u, dims, precision=HIGHEST, preferred_element_type=jnp.float32)
            s_ref[...] = pltpu.roll(s_new, RANK - SUPER, 1)
            a_ref[...] = a_ref[...] - lax.dot_general(back, ua, dims, precision=HIGHEST, preferred_element_type=jnp.float32)

        return carry

    lax.fori_loop(0, RANK // SUPER, group, 0)
    out_ref[...] = y_ref[...].T[0:64, :]


def finish(gram_tiles, rows):
    return pl.pallas_call(
        finish_kernel,
        out_shape=jax.ShapeDtypeStruct((64, RANK), jnp.float32),
        scratch_shapes=[
            pltpu.VMEM((RANK, RANK), jnp.float32),
            pltpu.VMEM((RANK, 128), jnp.float32),
            pltpu.VMEM((SUPER, RANK), jnp.float32),
            pltpu.VMEM((SUPER, 128), jnp.float32),
            pltpu.VMEM((RANK, 128), jnp.float32),
        ],
        name="finish",
    )(gram_tiles, rows)


def exchange(x, axes):
    return lax.all_to_all(x, axes, 0, 0, tiled=True)


def partner_pairs():
    size = 1
    for s in SIZES:
        size *= s
    return [(i, i ^ 8) for i in range(size)]


def body(tile_values, tile_row, tile_col, basis):
    core = lax.axis_index("core").astype(jnp.int32).reshape(1)
    keep, send = local_product(tile_values, tile_row, tile_col, basis, core)
    got = lax.ppermute(send, AXES, partner_pairs())
    both = keep + got
    over_x = jnp.sum(exchange(both, ("x",)), axis=0)
    over_zy = exchange(over_x.reshape(64, 8, RANK), ("z", "yh", "yl"))
    rows = exchange(sum_and_spread(over_zy, 8), ("yl", "x")).reshape(64, RANK)
    terms = exchange(gram_terms(rows), ("z", "yh", "core"))
    gram_tiles = exchange(sum_and_spread(terms, 64), ("z", "yh", "core"))
    return finish(gram_tiles, rows)


def solution(mesh):
    fine = Mesh(mesh.devices.reshape(SIZES), AXES)
    in_specs = (P(AXES, None, None), P(AXES), P(AXES), P(AXES, None))
    return jax.shard_map(
        body, mesh=fine, in_specs=in_specs, out_specs=P(("z", "yh", "core"), None), check_vma=False
    )
```

```python
import jax
import jax.numpy as jnp
from jax import lax
from jax.experimental import pallas as pl
from jax.experimental.pallas import tpu as pltpu
from jax.sharding import Mesh
from jax.sharding import PartitionSpec as P

AXES = ("zh", "zl", "yh", "core", "yl", "xh", "xl")
SIZES = (4, 2, 4, 2, 2, 2, 2)
NEAR = ("zl", "yl", "xl")
FAR = ("zh", "yh", "xh")
WIDE = ("zh", "zl", "yh", "core")
NARROW = ("yl", "xh", "xl")
TILE = 512
RANK = 256
COLS = 4096
HIGHEST = lax.Precision.HIGHEST
SUPER = 64
HALF = (8, 32, 8, RANK)
IN_VMEM = pl.BlockSpec(memory_space=pltpu.VMEM)


def held(x):
    return pltpu.with_memory_space_constraint(x, pltpu.VMEM)


def left_out(x):
    return pltpu.with_memory_space_constraint(x, pltpu.HBM)


def product_kernel(row_ref, col_ref, core_ref, tile_ref, basis_ref, keep_ref, send_ref, rounded):
    step = pl.program_id(0)

    @pl.when(step == 0)
    def _():
        rounded[...] = basis_ref[...].astype(jnp.bfloat16).reshape(rounded.shape)
        keep_ref[...] = jnp.zeros_like(keep_ref)
        send_ref[...] = jnp.zeros_like(send_ref)

    c = col_ref[step]
    near, far = (c % 2) * 4, (c // 2) * 8
    res = lax.dot_general(
        tile_ref[0],
        rounded[row_ref[step]],
        (((0,), (0,)), ((), ())),
        preferred_element_type=jnp.float32,
    )

    def add(halves):
        for yh in range(4):
            for core in range(2):
                for yl in range(2):
                    for xh in range(2):
                        for xl in range(2):
                            i = (((yh * 2 + core) * 2 + yl) * 2 + xh) * 2 + xl
                            halves[core][near + yl * 2 + xl, far + yh * 2 + xh] += res[8 * i : 8 * i + 8, :]

    @pl.when(core_ref[0] == 0)
    def _():
        add((keep_ref, send_ref))

    @pl.when(core_ref[0] == 1)
    def _():
        add((send_ref, keep_ref))


def local_product(tile_values, tile_row, tile_col, basis, core):
    tiles = tile_values.shape[0]
    blocks = basis.shape[0] // TILE
    return pl.pallas_call(
        product_kernel,
        grid_spec=pltpu.PrefetchScalarGridSpec(
            num_scalar_prefetch=3,
            grid=(tiles,),
            in_specs=[
                pl.BlockSpec((1, TILE, TILE), lambda t, *_: (t, 0, 0)),
                pl.BlockSpec(basis.shape, lambda t, *_: (0, 0)),
            ],
            out_specs=[IN_VMEM, IN_VMEM],
            scratch_shapes=[pltpu.VMEM((blocks, TILE, RANK), jnp.bfloat16)],
        ),
        out_shape=[pltpu.VMEM(HALF, jnp.float32)] * 2,
        compiler_params=pltpu.CompilerParams(vmem_limit_bytes=16 << 20),
        name="local_product",
    )(left_out(tile_row), left_out(tile_col), core, left_out(tile_values), left_out(basis))


def sum_and_spread(parts, copies):
    total = jnp.sum(parts, axis=0)
    return jnp.broadcast_to(total, (copies,) + total.shape)


def gram_kernel(rows_ref, out_ref):
    rows = rows_ref[...]
    gram = lax.dot_general(
        rows,
        rows,
        (((0,), (0,)), ((), ())),
        precision=HIGHEST,
        preferred_element_type=jnp.float32,
    )
    for i in range(RANK // 8):
        for h in range(2):
            out_ref[2 * i + h] = gram[8 * i : 8 * i + 8, 128 * h : 128 * h + 128]


def gram_terms(rows):
    return pl.pallas_call(
        gram_kernel,
        in_specs=[IN_VMEM],
        out_specs=IN_VMEM,
        out_shape=pltpu.VMEM((64, 8, 128), jnp.float32),
        compiler_params=pltpu.CompilerParams(vmem_limit_bytes=8 << 20),
        name="gram_terms",
    )(held(rows))


def lane(v, j):
    return jnp.broadcast_to(v[:, j : j + 1], (8, 128))


def sub(v, i):
    return jnp.broadcast_to(v[i : i + 1, :], v.shape)


def invert_factor(block, at):
    e = {}
    for j in range(8):
        column = lane(block, at + j)
        for i in range(j, 8):
            e[i, j] = sub(column, i)
    inv = {}
    for j in range(8):
        p = e[j, j]
        r = lax.rsqrt(p)
        r = r * (1.5 - 0.5 * (p * r) * r)
        inv[j, j] = r
        for i in range(j + 1, 8):
            e[i, j] = e[i, j] * r
        for k in range(j + 1, 8):
            for i in range(k, 8):
                e[i, k] = e[i, k] - e[i, j] * e[k, j]
    for i in range(1, 8):
        for j in range(i):
            acc = e[i, j] * inv[j, j]
            for k in range(j + 1, i):
                acc = acc + e[i, k] * inv[k, j]
            inv[i, j] = -acc * inv[i, i]
    place = lax.broadcasted_iota(jnp.int32, (8, 128), 0)
    zero = jnp.zeros((8, 128), jnp.float32)
    lower, upper = [], []
    for j in range(8):
        down = zero
        for i in range(j, 8):
            down = jnp.where(place == i, inv[i, j], down)
        lower.append(down)
        across = zero
        for i in range(j + 1):
            across = jnp.where(place == i, inv[j, i], across)
        upper.append(across)
    return lower, upper


def combine(columns, rows):
    out = []
    for piece in rows:
        acc = columns[0] * sub(piece, 0)
        for j in range(1, 8):
            acc = acc + columns[j] * sub(piece, j)
        out.append(acc)
    return out


def finish_kernel(gram_ref, rows_ref, out_ref, s_ref, a_ref, u_ref, ua_ref, y_ref):
    for i in range(RANK // 8):
        for h in range(2):
            s_ref[8 * i : 8 * i + 8, 128 * h : 128 * h + 128] = gram_ref[2 * i + h] * (1.0 / COLS)
    rows = rows_ref[...]
    a_ref[...] = jnp.concatenate([rows, jnp.zeros_like(rows)], axis=0).T

    def group(g, carry):
        first = pl.multiple_of(g * SUPER, SUPER)
        u_ref[...] = s_ref[pl.ds(first, SUPER), :]
        ua_ref[...] = a_ref[pl.ds(first, SUPER), :]
        panels = SUPER // 8
        for k in range(panels):
            here = slice(8 * k, 8 * k + 8)
            pieces = [u_ref[here, 0:128], u_ref[here, 128:256], ua_ref[here, :]]
            lower, upper = invert_factor(pieces[0], 8 * k)
            scaled = combine(lower, pieces)
            u_ref[here, 0:128] = scaled[0]
            u_ref[here, 128:256] = scaled[1]
            ua_ref[here, :] = scaled[2]
            if k + 1 < panels:
                w = combine(upper, scaled)
                wide_rows = [[sub(piece, j) for j in range(8)] for piece in w]
                for q in range(k + 1, panels):
                    there = slice(8 * q, 8 * q + 8)
                    old = [u_ref[there, 0:128], u_ref[there, 128:256], ua_ref[there, :]]
                    ms = [lane(old[0], 8 * k + j) for j in range(8)]
                    new = []
                    for piece, wr in zip(old, wide_rows):
                        acc = piece
                        for j in range(8):
                            acc = acc - ms[j] * wr[j]
                        new.append(acc)
                    u_ref[there, 0:128] = new[0]
                    u_ref[there, 128:256] = new[1]
                    ua_ref[there, :] = new[2]
        u, ua = u_ref[...], ua_ref[...]
        y_ref[pl.ds(first, SUPER), :] = ua

        @pl.when(g + 1 < RANK // SUPER)
        def _():
            dims = (((0,), (0,)), ((), ()))
            left = u
            back = pltpu.roll(left, first, 1)
            s_new = s_ref[...] - lax.dot_general(back, u, dims, precision=HIGHEST, preferred_element_type=jnp.float32)
            s_ref[...] = pltpu.roll(s_new, RANK - SUPER, 1)
            a_ref[...] = a_ref[...] - lax.dot_general(back, ua, dims, precision=HIGHEST, preferred_element_type=jnp.float32)

        return carry

    lax.fori_loop(0, RANK // SUPER, group, 0)
    out_ref[...] = y_ref[...].T[0:64, :]


def finish(gram_tiles, rows):
    return pl.pallas_call(
        finish_kernel,
        in_specs=[IN_VMEM, IN_VMEM],
        out_shape=jax.ShapeDtypeStruct((64, RANK), jnp.float32),
        scratch_shapes=[
            pltpu.VMEM((RANK, RANK), jnp.float32),
            pltpu.VMEM((RANK, 128), jnp.float32),
            pltpu.VMEM((SUPER, RANK), jnp.float32),
            pltpu.VMEM((SUPER, 128), jnp.float32),
            pltpu.VMEM((RANK, 128), jnp.float32),
        ],
        compiler_params=pltpu.CompilerParams(vmem_limit_bytes=8 << 20),
        name="finish",
    )(held(gram_tiles), held(rows))


def exchange(x, axes):
    return lax.all_to_all(x, axes, 0, 0, tiled=True)


def partner_pairs():
    return [(i, i ^ 8) for i in range(512)]


def body(tile_values, tile_row, tile_col, basis):
    core = lax.axis_index("core").astype(jnp.int32).reshape(1)
    keep, send = local_product(tile_values, tile_row, tile_col, basis, core)
    both = keep + lax.ppermute(send, AXES, partner_pairs())
    over_near = jnp.sum(exchange(both, NEAR), axis=0)
    rows = exchange(sum_and_spread(exchange(over_near, FAR), 8), NARROW).reshape(64, RANK)
    terms = exchange(gram_terms(rows), WIDE)
    gram_tiles = exchange(sum_and_spread(terms, 64), WIDE)
    return finish(gram_tiles, rows)


def solution(mesh):
    fine = Mesh(mesh.devices.reshape(SIZES), AXES)
    in_specs = (P(AXES, None, None), P(AXES), P(AXES), P(AXES, None))
    return jax.shard_map(
        body, mesh=fine, in_specs=in_specs, out_specs=P(WIDE, None), check_vma=False
    )
```

```python
import itertools
import math

import jax
import jax.numpy as jnp
import numpy as np
from jax import lax
from jax.experimental import pallas as pl
from jax.experimental.pallas import tpu as pltpu
from jax.sharding import PartitionSpec as P

AXES = ("zh", "zl", "yh", "core", "yl", "xh", "xl")
SIZES = (4, 2, 4, 2, 2, 2, 2)
ALL = ("wide", "narrow")
FAR = ("zh", "yh", "xh")
WIDE = ("zh", "zl", "yh", "core")
NARROW = ("yl", "xh", "xl")
TILE = 512
RANK = 256
COLS = 4096
HIGHEST = lax.Precision.HIGHEST
SUPER = 64
HALF = (8, 32, 8, RANK)
IN_VMEM = pl.BlockSpec(memory_space=pltpu.VMEM)


def held(x):
    return pltpu.with_memory_space_constraint(x, pltpu.VMEM)


def left_out(x):
    return pltpu.with_memory_space_constraint(x, pltpu.HBM)


def product_kernel(row_ref, col_ref, core_ref, tile_ref, basis_ref, keep_ref, send_ref, rounded):
    step = pl.program_id(0)

    @pl.when(step == 0)
    def _():
        rounded[...] = basis_ref[...].astype(jnp.bfloat16).reshape(rounded.shape)
        keep_ref[...] = jnp.zeros_like(keep_ref)
        send_ref[...] = jnp.zeros_like(send_ref)

    c = col_ref[step]
    near, far = (c % 2) * 4, (c // 2) * 8
    res = lax.dot_general(
        tile_ref[0],
        rounded[row_ref[step]],
        (((0,), (0,)), ((), ())),
        preferred_element_type=jnp.float32,
    )

    def add(halves):
        for yh in range(4):
            for core in range(2):
                for yl in range(2):
                    for xh in range(2):
                        for xl in range(2):
                            i = (((yh * 2 + core) * 2 + yl) * 2 + xh) * 2 + xl
                            halves[core][near + yl * 2 + xl, far + yh * 2 + xh] += res[8 * i : 8 * i + 8, :]

    @pl.when(core_ref[0] == 0)
    def _():
        add((keep_ref, send_ref))

    @pl.when(core_ref[0] == 1)
    def _():
        add((send_ref, keep_ref))


def local_product(tile_values, tile_row, tile_col, basis, core):
    tiles = tile_values.shape[0]
    blocks = basis.shape[0] // TILE
    return pl.pallas_call(
        product_kernel,
        grid_spec=pltpu.PrefetchScalarGridSpec(
            num_scalar_prefetch=3,
            grid=(tiles,),
            in_specs=[
                pl.BlockSpec((1, TILE, TILE), lambda t, *_: (t, 0, 0)),
                pl.BlockSpec(basis.shape, lambda t, *_: (0, 0)),
            ],
            out_specs=[IN_VMEM, IN_VMEM],
            scratch_shapes=[pltpu.VMEM((blocks, TILE, RANK), jnp.bfloat16)],
        ),
        out_shape=[pltpu.VMEM(HALF, jnp.float32)] * 2,
        compiler_params=pltpu.CompilerParams(vmem_limit_bytes=16 << 20),
        name="local_product",
    )(left_out(tile_row), left_out(tile_col), core, left_out(tile_values), left_out(basis))


def sum_and_spread(parts, copies):
    total = jnp.sum(parts, axis=0)
    return jnp.broadcast_to(total, (copies,) + total.shape)


def gram_kernel(rows_ref, out_ref):
    rows = rows_ref[...]
    gram = lax.dot_general(
        rows,
        rows,
        (((0,), (0,)), ((), ())),
        precision=HIGHEST,
        preferred_element_type=jnp.float32,
    )
    for i in range(RANK // 8):
        for h in range(2):
            out_ref[2 * i + h] = gram[8 * i : 8 * i + 8, 128 * h : 128 * h + 128]


def gram_terms(rows):
    return pl.pallas_call(
        gram_kernel,
        in_specs=[IN_VMEM],
        out_specs=IN_VMEM,
        out_shape=pltpu.VMEM((64, 8, 128), jnp.float32),
        compiler_params=pltpu.CompilerParams(vmem_limit_bytes=8 << 20),
        name="gram_terms",
    )(held(rows))


def lane(v, j):
    return jnp.broadcast_to(v[:, j : j + 1], (8, 128))


def sub(v, i):
    return jnp.broadcast_to(v[i : i + 1, :], v.shape)


def invert_factor(block, at):
    e = {}
    for j in range(8):
        column = lane(block, at + j)
        for i in range(j, 8):
            e[i, j] = sub(column, i)
    inv = {}
    for j in range(8):
        p = e[j, j]
        r = lax.rsqrt(p)
        r = r * (1.5 - 0.5 * (p * r) * r)
        inv[j, j] = r
        for i in range(j + 1, 8):
            e[i, j] = e[i, j] * r
        for k in range(j + 1, 8):
            for i in range(k, 8):
                e[i, k] = e[i, k] - e[i, j] * e[k, j]
    for i in range(1, 8):
        for j in range(i):
            acc = e[i, j] * inv[j, j]
            for k in range(j + 1, i):
                acc = acc + e[i, k] * inv[k, j]
            inv[i, j] = -acc * inv[i, i]
    place = lax.broadcasted_iota(jnp.int32, (8, 128), 0)
    zero = jnp.zeros((8, 128), jnp.float32)
    lower, upper = [], []
    for j in range(8):
        down = zero
        for i in range(j, 8):
            down = jnp.where(place == i, inv[i, j], down)
        lower.append(down)
        across = zero
        for i in range(j + 1):
            across = jnp.where(place == i, inv[j, i], across)
        upper.append(across)
    return lower, upper


def combine(columns, rows):
    out = []
    for piece in rows:
        acc = columns[0] * sub(piece, 0)
        for j in range(1, 8):
            acc = acc + columns[j] * sub(piece, j)
        out.append(acc)
    return out


def finish_kernel(gram_ref, rows_ref, out_ref, s_ref, a_ref, u_ref, ua_ref, y_ref):
    for i in range(RANK // 8):
        for h in range(2):
            s_ref[8 * i : 8 * i + 8, 128 * h : 128 * h + 128] = gram_ref[2 * i + h] * (1.0 / COLS)
    rows = rows_ref[...]
    a_ref[...] = jnp.concatenate([rows, jnp.zeros_like(rows)], axis=0).T

    def group(g, carry):
        first = pl.multiple_of(g * SUPER, SUPER)
        u_ref[...] = s_ref[pl.ds(first, SUPER), :]
        ua_ref[...] = a_ref[pl.ds(first, SUPER), :]
        panels = SUPER // 8
        for k in range(panels):
            here = slice(8 * k, 8 * k + 8)
            pieces = [u_ref[here, 0:128], u_ref[here, 128:256], ua_ref[here, :]]
            lower, upper = invert_factor(pieces[0], 8 * k)
            scaled = combine(lower, pieces)
            u_ref[here, 0:128] = scaled[0]
            u_ref[here, 128:256] = scaled[1]
            ua_ref[here, :] = scaled[2]
            if k + 1 < panels:
                w = combine(upper, scaled)
                wide_rows = [[sub(piece, j) for j in range(8)] for piece in w]
                for q in range(k + 1, panels):
                    there = slice(8 * q, 8 * q + 8)
                    old = [u_ref[there, 0:128], u_ref[there, 128:256], ua_ref[there, :]]
                    ms = [lane(old[0], 8 * k + j) for j in range(8)]
                    new = []
                    for piece, wr in zip(old, wide_rows):
                        acc = piece
                        for j in range(8):
                            acc = acc - ms[j] * wr[j]
                        new.append(acc)
                    u_ref[there, 0:128] = new[0]
                    u_ref[there, 128:256] = new[1]
                    ua_ref[there, :] = new[2]
        u, ua = u_ref[...], ua_ref[...]
        y_ref[pl.ds(first, SUPER), :] = ua

        @pl.when(g + 1 < RANK // SUPER)
        def _():
            dims = (((0,), (0,)), ((), ()))
            left = u
            back = pltpu.roll(left, first, 1)
            s_new = s_ref[...] - lax.dot_general(back, u, dims, precision=HIGHEST, preferred_element_type=jnp.float32)
            s_ref[...] = pltpu.roll(s_new, RANK - SUPER, 1)
            a_ref[...] = a_ref[...] - lax.dot_general(back, ua, dims, precision=HIGHEST, preferred_element_type=jnp.float32)

        return carry

    lax.fori_loop(0, RANK // SUPER, group, 0)
    out_ref[...] = y_ref[...].T[0:64, :]


def finish(gram_tiles, rows):
    return pl.pallas_call(
        finish_kernel,
        in_specs=[IN_VMEM, IN_VMEM],
        out_shape=jax.ShapeDtypeStruct((64, RANK), jnp.float32),
        scratch_shapes=[
            pltpu.VMEM((RANK, RANK), jnp.float32),
            pltpu.VMEM((RANK, 128), jnp.float32),
            pltpu.VMEM((SUPER, RANK), jnp.float32),
            pltpu.VMEM((SUPER, 128), jnp.float32),
            pltpu.VMEM((RANK, 128), jnp.float32),
        ],
        compiler_params=pltpu.CompilerParams(vmem_limit_bytes=8 << 20),
        name="finish",
    )(held(gram_tiles), held(rows))


def members(axes):
    index = np.arange(512).reshape(SIZES)
    inner = [AXES.index(a) for a in axes]
    outer = [i for i in range(len(AXES)) if i not in inner]
    count = math.prod(SIZES[i] for i in inner)
    return index.transpose(outer + inner).reshape(-1, count).tolist()


def cubes():
    groups = []
    for core in range(2):
        for z, y, x in itertools.product(range(0, 8, 2), range(0, 8, 2), range(0, 4, 2)):
            group = [0] * 8
            for dz, dy, dx in itertools.product(range(2), repeat=3):
                at = ((z + core + dz) % 8, (y + core + dy) % 8, (x + core + dx) % 4)
                place = (at[0] % 2) * 4 + (at[1] % 2) * 2 + at[2] % 2
                group[place] = ((at[0] * 4 + at[1] // 2) * 2 + core) * 8 + (at[1] % 2) * 4 + at[2]
            groups.append(group)
    return groups


def exchange(x, groups):
    return lax.all_to_all(x, ALL, 0, 0, axis_index_groups=groups, tiled=True)


def partner_pairs():
    return [(i, i ^ 8) for i in range(512)]


def body(tile_values, tile_row, tile_col, basis):
    core = (lax.axis_index("wide").astype(jnp.int32) & 1).reshape(1)
    wide, narrow = members(WIDE), members(NARROW)
    keep, send = local_product(tile_values, tile_row, tile_col, basis, core)
    both = keep + lax.ppermute(send, ALL, partner_pairs())
    over_near = jnp.sum(exchange(both, cubes()), axis=0)
    rows = exchange(sum_and_spread(exchange(over_near, members(FAR)), 8), narrow).reshape(64, RANK)
    terms = exchange(gram_terms(rows), wide)
    gram_tiles = exchange(sum_and_spread(terms, 64), wide)
    return finish(gram_tiles, rows)


def solution(mesh):
    axes = mesh.axis_names
    in_specs = (P(axes, None, None), P(axes), P(axes), P(axes, None))
    return jax.shard_map(body, mesh=mesh, in_specs=in_specs, out_specs=P("wide", None), check_vma=False)
```

```python
import itertools
import math

import jax
import jax.numpy as jnp
import numpy as np
from jax import lax
from jax.experimental import pallas as pl
from jax.experimental.pallas import tpu as pltpu
from jax.sharding import PartitionSpec as P

AXES = ("zh", "zl", "yh", "core", "yl", "xh", "xl")
SIZES = (4, 2, 4, 2, 2, 2, 2)
ALL = ("wide", "narrow")
FAR = ("zh", "yh", "xh")
TILE = 512
RANK = 256
COLS = 4096
HIGHEST = lax.Precision.HIGHEST
SUPER = 64
HALF = (8, 32, 8, RANK)
IN_VMEM = pl.BlockSpec(memory_space=pltpu.VMEM)


def held(x):
    return pltpu.with_memory_space_constraint(x, pltpu.VMEM)


def left_out(x):
    return pltpu.with_memory_space_constraint(x, pltpu.HBM)


def product_kernel(row_ref, col_ref, core_ref, tile_ref, basis_ref, keep_ref, send_ref, rounded):
    step = pl.program_id(0)

    @pl.when(step == 0)
    def _():
        rounded[...] = basis_ref[...].astype(jnp.bfloat16).reshape(rounded.shape)
        keep_ref[...] = jnp.zeros_like(keep_ref)
        send_ref[...] = jnp.zeros_like(send_ref)

    c = col_ref[step]
    near, far = (c % 2) * 4, (c // 2) * 8
    res = lax.dot_general(
        tile_ref[0],
        rounded[row_ref[step]],
        (((0,), (0,)), ((), ())),
        preferred_element_type=jnp.float32,
    )

    def add(halves):
        for yh in range(4):
            for core in range(2):
                for yl in range(2):
                    for xh in range(2):
                        for xl in range(2):
                            i = (((yh * 2 + core) * 2 + yl) * 2 + xh) * 2 + xl
                            halves[core][near + yl * 2 + xl, far + yh * 2 + xh] += res[8 * i : 8 * i + 8, :]

    @pl.when(core_ref[0] == 0)
    def _():
        add((keep_ref, send_ref))

    @pl.when(core_ref[0] == 1)
    def _():
        add((send_ref, keep_ref))


def local_product(tile_values, tile_row, tile_col, basis, core):
    tiles = tile_values.shape[0]
    blocks = basis.shape[0] // TILE
    return pl.pallas_call(
        product_kernel,
        grid_spec=pltpu.PrefetchScalarGridSpec(
            num_scalar_prefetch=3,
            grid=(tiles,),
            in_specs=[
                pl.BlockSpec((1, TILE, TILE), lambda t, *_: (t, 0, 0)),
                pl.BlockSpec(basis.shape, lambda t, *_: (0, 0)),
            ],
            out_specs=[IN_VMEM, IN_VMEM],
            scratch_shapes=[pltpu.VMEM((blocks, TILE, RANK), jnp.bfloat16)],
        ),
        out_shape=[pltpu.VMEM(HALF, jnp.float32)] * 2,
        compiler_params=pltpu.CompilerParams(vmem_limit_bytes=16 << 20),
        name="local_product",
    )(left_out(tile_row), left_out(tile_col), core, left_out(tile_values), left_out(basis))


def sum_and_spread(parts, copies):
    total = jnp.sum(parts, axis=0)
    return jnp.broadcast_to(total, (copies,) + total.shape)


def gram_kernel(rows_ref, out_ref):
    rows = rows_ref[...]
    out_ref[...] = lax.dot_general(
        rows,
        rows,
        (((0,), (0,)), ((), ())),
        precision=HIGHEST,
        preferred_element_type=jnp.float32,
    )


def gram_terms(rows):
    return pl.pallas_call(
        gram_kernel,
        in_specs=[IN_VMEM],
        out_specs=IN_VMEM,
        out_shape=pltpu.VMEM((RANK, RANK), jnp.float32),
        compiler_params=pltpu.CompilerParams(vmem_limit_bytes=24 << 20),
        name="gram_terms",
    )(held(rows))


def lane(v, j):
    return jnp.broadcast_to(v[:, j : j + 1], (8, 128))


def sub(v, i):
    return jnp.broadcast_to(v[i : i + 1, :], v.shape)


def invert_factor(block, at):
    e = {}
    for j in range(8):
        column = lane(block, at + j)
        for i in range(j, 8):
            e[i, j] = sub(column, i)
    inv = {}
    for j in range(8):
        p = e[j, j]
        r = lax.rsqrt(p)
        r = r * (1.5 - 0.5 * (p * r) * r)
        inv[j, j] = r
        for i in range(j + 1, 8):
            e[i, j] = e[i, j] * r
        for k in range(j + 1, 8):
            for i in range(k, 8):
                e[i, k] = e[i, k] - e[i, j] * e[k, j]
    for i in range(1, 8):
        for j in range(i):
            acc = e[i, j] * inv[j, j]
            for k in range(j + 1, i):
                acc = acc + e[i, k] * inv[k, j]
            inv[i, j] = -acc * inv[i, i]
    place = lax.broadcasted_iota(jnp.int32, (8, 128), 0)
    zero = jnp.zeros((8, 128), jnp.float32)
    lower, upper = [], []
    for j in range(8):
        down = zero
        for i in range(j, 8):
            down = jnp.where(place == i, inv[i, j], down)
        lower.append(down)
        across = zero
        for i in range(j + 1):
            across = jnp.where(place == i, inv[j, i], across)
        upper.append(across)
    return lower, upper


def combine(columns, rows):
    out = []
    for piece in rows:
        acc = columns[0] * sub(piece, 0)
        for j in range(1, 8):
            acc = acc + columns[j] * sub(piece, j)
        out.append(acc)
    return out


def finish_kernel(at_ref, gram_ref, other_ref, rows_ref, out_ref, s_ref, a_ref, u_ref, ua_ref, y_ref):
    s_ref[...] = (gram_ref[...] + other_ref[...]) * (1.0 / COLS)
    zl, far = at_ref[0], at_ref[1]
    rows = jnp.concatenate(
        [
            rows_ref[zl * 4 + yl * 2 + xl, far + xh]
            for yl in range(2)
            for xh in range(2)
            for xl in range(2)
        ],
        axis=0,
    )
    a_ref[...] = jnp.concatenate([rows, jnp.zeros_like(rows)], axis=0).T

    def group(g, carry):
        first = pl.multiple_of(g * SUPER, SUPER)
        u_ref[...] = s_ref[pl.ds(first, SUPER), :]
        ua_ref[...] = a_ref[pl.ds(first, SUPER), :]
        panels = SUPER // 8
        for k in range(panels):
            here = slice(8 * k, 8 * k + 8)
            pieces = [u_ref[here, 0:128], u_ref[here, 128:256], ua_ref[here, :]]
            lower, upper = invert_factor(pieces[0], 8 * k)
            scaled = combine(lower, pieces)
            u_ref[here, 0:128] = scaled[0]
            u_ref[here, 128:256] = scaled[1]
            ua_ref[here, :] = scaled[2]
            if k + 1 < panels:
                w = combine(upper, scaled)
                wide_rows = [[sub(piece, j) for j in range(8)] for piece in w]
                for q in range(k + 1, panels):
                    there = slice(8 * q, 8 * q + 8)
                    old = [u_ref[there, 0:128], u_ref[there, 128:256], ua_ref[there, :]]
                    ms = [lane(old[0], 8 * k + j) for j in range(8)]
                    new = []
                    for piece, wr in zip(old, wide_rows):
                        acc = piece
                        for j in range(8):
                            acc = acc - ms[j] * wr[j]
                        new.append(acc)
                    u_ref[there, 0:128] = new[0]
                    u_ref[there, 128:256] = new[1]
                    ua_ref[there, :] = new[2]
        u, ua = u_ref[...], ua_ref[...]
        y_ref[pl.ds(first, SUPER), :] = ua

        @pl.when(g + 1 < RANK // SUPER)
        def _():
            dims = (((0,), (0,)), ((), ()))
            left = u
            back = pltpu.roll(left, first, 1)
            s_new = s_ref[...] - lax.dot_general(back, u, dims, precision=HIGHEST, preferred_element_type=jnp.float32)
            s_ref[...] = pltpu.roll(s_new, RANK - SUPER, 1)
            a_ref[...] = a_ref[...] - lax.dot_general(back, ua, dims, precision=HIGHEST, preferred_element_type=jnp.float32)

        return carry

    lax.fori_loop(0, RANK // SUPER, group, 0)
    out_ref[...] = y_ref[...].T[0:64, :]


def finish(at, gram, other, rows):
    return pl.pallas_call(
        finish_kernel,
        in_specs=[pl.BlockSpec(memory_space=pltpu.SMEM), IN_VMEM, IN_VMEM, IN_VMEM],
        out_shape=jax.ShapeDtypeStruct((64, RANK), jnp.float32),
        scratch_shapes=[
            pltpu.VMEM((RANK, RANK), jnp.float32),
            pltpu.VMEM((RANK, 128), jnp.float32),
            pltpu.VMEM((SUPER, RANK), jnp.float32),
            pltpu.VMEM((SUPER, 128), jnp.float32),
            pltpu.VMEM((RANK, 128), jnp.float32),
        ],
        compiler_params=pltpu.CompilerParams(vmem_limit_bytes=12 << 20),
        name="finish",
    )(at, held(gram), held(other), held(rows))


def members(axes):
    index = np.arange(512).reshape(SIZES)
    inner = [AXES.index(a) for a in axes]
    outer = [i for i in range(len(AXES)) if i not in inner]
    count = math.prod(SIZES[i] for i in inner)
    return index.transpose(outer + inner).reshape(-1, count).tolist()


def cubes():
    groups = []
    for core in range(2):
        for z, y, x in itertools.product(range(0, 8, 2), range(0, 8, 2), range(0, 4, 2)):
            group = [0] * 8
            for dz, dy, dx in itertools.product(range(2), repeat=3):
                at = ((z + core + dz) % 8, (y + core + dy) % 8, (x + core + dx) % 4)
                place = (at[0] % 2) * 4 + (at[1] % 2) * 2 + at[2] % 2
                group[place] = ((at[0] * 4 + at[1] // 2) * 2 + core) * 8 + (at[1] % 2) * 4 + at[2]
            groups.append(group)
    return groups


def exchange(x, groups):
    return lax.all_to_all(x, ALL, 0, 0, axis_index_groups=groups, tiled=True)


PARTNERS = [(i, i ^ 8) for i in range(512)]


def body(tile_values, tile_row, tile_col, basis):
    wide = lax.axis_index("wide").astype(jnp.int32)
    core, z, yh = wide & 1, wide >> 3, (wide >> 1) & 3
    near, far = cubes(), members(FAR)
    keep, send = local_product(tile_values, tile_row, tile_col, basis, core.reshape(1))
    both = keep + lax.ppermute(send, ALL, PARTNERS)
    over_near = jnp.sum(exchange(both, near), axis=0)
    far_rows = exchange(sum_and_spread(exchange(over_near, far), 32), far)
    rows = exchange(jnp.broadcast_to(far_rows, HALF), near)
    gram = gram_terms(rows.reshape(COLS // 2, RANK))
    other = lax.ppermute(gram, ALL, PARTNERS)
    at = jnp.stack([z & 1, (z >> 1) * 8 + yh * 2])
    return finish(at, gram, other, rows)


def solution(mesh):
    axes = mesh.axis_names
    in_specs = (P(axes, None, None), P(axes), P(axes), P(axes, None))
    return jax.shard_map(body, mesh=mesh, in_specs=in_specs, out_specs=P("wide", None), check_vma=False)
```

```python
import itertools
import math

import jax
import jax.numpy as jnp
import numpy as np
from jax import lax
from jax.experimental import pallas as pl
from jax.experimental.pallas import tpu as pltpu
from jax.sharding import PartitionSpec as P

AXES = ("zh", "zl", "yh", "core", "yl", "xh", "xl")
SIZES = (4, 2, 4, 2, 2, 2, 2)
ALL = ("wide", "narrow")
FAR = ("zh", "yh", "xh")
TILE = 512
RANK = 256
COLS = 4096
HIGHEST = lax.Precision.HIGHEST
HALF = (8, 32, 8, RANK)
IN_VMEM = pl.BlockSpec(memory_space=pltpu.VMEM)


def held(x):
    return pltpu.with_memory_space_constraint(x, pltpu.VMEM)


def left_out(x):
    return pltpu.with_memory_space_constraint(x, pltpu.HBM)


def product_kernel(row_ref, col_ref, core_ref, tile_ref, basis_ref, keep_ref, send_ref, tiles, rows, rounded, tile_sem, row_sem):
    count = tiles.shape[0]
    rows_in = pltpu.make_async_copy(basis_ref, rows, row_sem)
    rows_in.start()
    for t in range(count):
        pltpu.make_async_copy(tile_ref.at[t], tiles.at[t], tile_sem.at[t]).start()
    keep_ref[...] = jnp.zeros_like(keep_ref)
    send_ref[...] = jnp.zeros_like(send_ref)
    rows_in.wait()
    rounded[...] = rows[...].astype(jnp.bfloat16).reshape(rounded.shape)

    def step(t, carry):
        pltpu.make_async_copy(tile_ref.at[t], tiles.at[t], tile_sem.at[t]).wait()
        c = col_ref[t]
        near, far = (c & 1) * 4, (c >> 1) * 8
        res = lax.dot_general(
            tiles[t],
            rounded[row_ref[t]],
            (((0,), (0,)), ((), ())),
            preferred_element_type=jnp.float32,
        )

        def add(halves):
            for yh in range(4):
                for core in range(2):
                    for yl in range(2):
                        for xh in range(2):
                            for xl in range(2):
                                i = (((yh * 2 + core) * 2 + yl) * 2 + xh) * 2 + xl
                                halves[core][near + yl * 2 + xl, far + yh * 2 + xh] += res[8 * i : 8 * i + 8, :]

        @pl.when(core_ref[0] == 0)
        def _():
            add((keep_ref, send_ref))

        @pl.when(core_ref[0] == 1)
        def _():
            add((send_ref, keep_ref))

        return carry

    lax.fori_loop(0, count, step, 0)


def local_product(tile_values, tile_row, tile_col, basis, core):
    tiles = tile_values.shape[0]
    blocks = basis.shape[0] // TILE
    outside = pl.BlockSpec(memory_space=pltpu.HBM)
    return pl.pallas_call(
        product_kernel,
        grid_spec=pltpu.PrefetchScalarGridSpec(
            num_scalar_prefetch=3,
            grid=(),
            in_specs=[outside, outside],
            out_specs=[IN_VMEM, IN_VMEM],
            scratch_shapes=[
                pltpu.VMEM(tile_values.shape, tile_values.dtype),
                pltpu.VMEM(basis.shape, basis.dtype),
                pltpu.VMEM((blocks, TILE, RANK), jnp.bfloat16),
                pltpu.SemaphoreType.DMA((tiles,)),
                pltpu.SemaphoreType.DMA,
            ],
        ),
        out_shape=[pltpu.VMEM(HALF, jnp.float32)] * 2,
        compiler_params=pltpu.CompilerParams(vmem_limit_bytes=16 << 20),
        name="local_product",
    )(left_out(tile_row), left_out(tile_col), core, left_out(tile_values), left_out(basis))


def sum_and_spread(parts, copies):
    total = jnp.sum(parts, axis=0)
    return jnp.broadcast_to(total, (copies,) + total.shape)


def gram_kernel(rows_ref, out_ref):
    rows = rows_ref[...]
    out_ref[...] = lax.dot_general(
        rows,
        rows,
        (((0,), (0,)), ((), ())),
        precision=HIGHEST,
        preferred_element_type=jnp.float32,
    )


def gram_terms(rows):
    return pl.pallas_call(
        gram_kernel,
        in_specs=[IN_VMEM],
        out_specs=IN_VMEM,
        out_shape=pltpu.VMEM((RANK, RANK), jnp.float32),
        compiler_params=pltpu.CompilerParams(vmem_limit_bytes=24 << 20),
        name="gram_terms",
    )(held(rows))


def lane(v, j):
    return jnp.broadcast_to(v[:, j : j + 1], (8, 128))


def sub(v, i):
    return jnp.broadcast_to(v[i : i + 1, :], v.shape)


def total(terms):
    while len(terms) > 1:
        terms = [x + y for x, y in zip(terms[::2], terms[1::2])] + terms[len(terms) & ~1 :]
    return terms[0]


def invert_factor(block, at):
    e = {}
    for j in range(8):
        column = lane(block, at + j)
        for i in range(j, 8):
            e[i, j] = sub(column, i)
    inv = {}
    for j in range(8):
        r = lax.rsqrt(e[j, j])
        inv[j, j] = r
        for i in range(j + 1, 8):
            e[i, j] = e[i, j] * r
        for k in range(j + 1, 8):
            for i in range(k, 8):
                e[i, k] = e[i, k] - e[i, j] * e[k, j]
        for k in range(j):
            inv[j, k] = -r * total([e[j, i] * inv[i, k] for i in range(k, j)])
    place = lax.broadcasted_iota(jnp.int32, (8, 128), 0)
    zero = jnp.zeros((8, 128), jnp.float32)
    lower, upper = [], []
    for j in range(8):
        down = across = zero
        for i in range(j, 8):
            down = jnp.where(place == i, inv[i, j], down)
        for i in range(j + 1):
            across = jnp.where(place == i, inv[j, i], across)
        lower.append(down)
        upper.append(across)
    return lower, upper


def combine(columns, rows):
    return [total([columns[j] * sub(piece, j) for j in range(8)]) for piece in rows]


def eliminate(refs, first):
    for k in range(16):
        here = slice(first + 8 * k, first + 8 * k + 8)
        pieces = [ref[here, :] for ref in refs]
        lower, upper = invert_factor(pieces[0], 8 * k)
        scaled = combine(lower, pieces)
        for ref, piece in zip(refs[1:], scaled[1:]):
            ref[here, :] = piece
        if k == 15:
            break
        solved = combine(upper, scaled)
        solved = [[sub(piece, j) for j in range(8)] for piece in solved]
        for q in range(k + 1, 16):
            there = slice(first + 8 * q, first + 8 * q + 8)
            old = [ref[there, :] for ref in refs]
            ms = [lane(old[0], 8 * k + j) for j in range(8)]
            for ref, piece, by in zip(refs, old, solved):
                ref[there, :] = piece - total([ms[j] * by[j] for j in range(8)])


def finish_kernel(at_ref, gram_ref, other_ref, rows_ref, out_ref, left_ref, right_ref, y_ref):
    s = (gram_ref[...] + other_ref[...]) * (1.0 / COLS)
    left_ref[...] = s[:, 0:128]
    right_ref[...] = s[:, 128:256]
    zl, far = at_ref[0], at_ref[1]
    rows = jnp.concatenate(
        [
            rows_ref[zl * 4 + yl * 2 + xl, far + xh]
            for yl in range(2)
            for xh in range(2)
            for xl in range(2)
        ],
        axis=0,
    )
    y_ref[...] = jnp.concatenate([rows, jnp.zeros_like(rows)], axis=0).T
    eliminate((left_ref, right_ref, y_ref), 0)
    u, ua = right_ref[0:128, :], y_ref[0:128, :]
    for ref, by in ((right_ref, u), (y_ref, ua)):
        ref[128:256, :] -= lax.dot_general(
            u, by, (((0,), (0,)), ((), ())), precision=HIGHEST, preferred_element_type=jnp.float32
        )
    eliminate((right_ref, y_ref), 128)
    out_ref[...] = y_ref[...].T[0:64, :]


def finish(at, gram, other, rows):
    return pl.pallas_call(
        finish_kernel,
        in_specs=[pl.BlockSpec(memory_space=pltpu.SMEM), IN_VMEM, IN_VMEM, IN_VMEM],
        out_shape=jax.ShapeDtypeStruct((64, RANK), jnp.float32),
        scratch_shapes=[pltpu.VMEM((RANK, 128), jnp.float32)] * 3,
        compiler_params=pltpu.CompilerParams(vmem_limit_bytes=12 << 20),
        name="finish",
    )(at, held(gram), held(other), held(rows))


def members(axes):
    index = np.arange(512).reshape(SIZES)
    inner = [AXES.index(a) for a in axes]
    outer = [i for i in range(len(AXES)) if i not in inner]
    count = math.prod(SIZES[i] for i in inner)
    return index.transpose(outer + inner).reshape(-1, count).tolist()


def cubes():
    groups = []
    for core in range(2):
        for z, y, x in itertools.product(range(0, 8, 2), range(0, 8, 2), range(0, 4, 2)):
            group = [0] * 8
            for dz, dy, dx in itertools.product(range(2), repeat=3):
                at = ((z + core + dz) % 8, (y + core + dy) % 8, (x + core + dx) % 4)
                place = (at[0] % 2) * 4 + (at[1] % 2) * 2 + at[2] % 2
                group[place] = ((at[0] * 4 + at[1] // 2) * 2 + core) * 8 + (at[1] % 2) * 4 + at[2]
            groups.append(group)
    return groups


def exchange(x, groups):
    return lax.all_to_all(x, ALL, 0, 0, axis_index_groups=groups, tiled=True)


PARTNERS = [(i, i ^ 8) for i in range(512)]


def body(tile_values, tile_row, tile_col, basis):
    wide = lax.axis_index("wide").astype(jnp.int32)
    core, z, yh = wide & 1, wide >> 3, (wide >> 1) & 3
    near, far = cubes(), members(FAR)
    keep, send = local_product(tile_values, tile_row, tile_col, basis, core.reshape(1))
    both = keep + lax.ppermute(send, ALL, PARTNERS)
    over_near = jnp.sum(exchange(both, near), axis=0)
    far_rows = exchange(sum_and_spread(exchange(over_near, far), 32), far)
    rows = exchange(jnp.broadcast_to(far_rows, HALF), near)
    gram = gram_terms(rows.reshape(COLS // 2, RANK))
    other = lax.ppermute(gram, ALL, PARTNERS)
    at = jnp.stack([z & 1, (z >> 1) * 8 + yh * 2])
    return finish(at, gram, other, rows)


def solution(mesh):
    axes = mesh.axis_names
    in_specs = (P(axes, None, None), P(axes), P(axes), P(axes, None))
    return jax.shard_map(body, mesh=mesh, in_specs=in_specs, out_specs=P("wide", None), check_vma=False)
```

```python
import itertools
import math

import jax
import jax.numpy as jnp
import numpy as np
from jax import lax
from jax.experimental import pallas as pl
from jax.experimental.pallas import tpu as pltpu
from jax.sharding import PartitionSpec as P

AXES = ("zh", "zl", "yh", "core", "yl", "xh", "xl")
SIZES = (4, 2, 4, 2, 2, 2, 2)
ALL = ("wide", "narrow")
FAR = ("zh", "yh", "xh")
TILE = 512
RANK = 256
COLS = 4096
HIGHEST = lax.Precision.HIGHEST
HALF = (8, 32, 8, RANK)
IN_VMEM = pl.BlockSpec(memory_space=pltpu.VMEM)


def held(x):
    return pltpu.with_memory_space_constraint(x, pltpu.VMEM)


def left_out(x):
    return pltpu.with_memory_space_constraint(x, pltpu.HBM)


def product_kernel(row_ref, col_ref, core_ref, tile_ref, basis_ref, keep_ref, send_ref, tiles, rows, rounded, tile_sem, row_sem):
    count = tiles.shape[0]
    rows_in = pltpu.make_async_copy(basis_ref, rows, row_sem)
    rows_in.start()
    for t in range(count):
        pltpu.make_async_copy(tile_ref.at[t], tiles.at[t], tile_sem.at[t]).start()
    keep_ref[...] = jnp.zeros_like(keep_ref)
    send_ref[...] = jnp.zeros_like(send_ref)
    rows_in.wait()
    rounded[...] = rows[...].astype(jnp.bfloat16).reshape(rounded.shape)

    def step(t, carry):
        pltpu.make_async_copy(tile_ref.at[t], tiles.at[t], tile_sem.at[t]).wait()
        c = col_ref[t]
        near, far = (c & 1) * 4, (c >> 1) * 8
        res = lax.dot_general(
            tiles[t],
            rounded[row_ref[t]],
            (((0,), (0,)), ((), ())),
            preferred_element_type=jnp.float32,
        )

        def add(halves):
            for yh in range(4):
                for core in range(2):
                    for yl in range(2):
                        for xh in range(2):
                            for xl in range(2):
                                i = (((yh * 2 + core) * 2 + yl) * 2 + xh) * 2 + xl
                                halves[core][near + yl * 2 + xl, far + yh * 2 + xh] += res[8 * i : 8 * i + 8, :]

        @pl.when(core_ref[0] == 0)
        def _():
            add((keep_ref, send_ref))

        @pl.when(core_ref[0] == 1)
        def _():
            add((send_ref, keep_ref))

        return carry

    lax.fori_loop(0, count, step, 0)


def local_product(tile_values, tile_row, tile_col, basis, core):
    tiles = tile_values.shape[0]
    blocks = basis.shape[0] // TILE
    outside = pl.BlockSpec(memory_space=pltpu.HBM)
    return pl.pallas_call(
        product_kernel,
        grid_spec=pltpu.PrefetchScalarGridSpec(
            num_scalar_prefetch=3,
            grid=(),
            in_specs=[outside, outside],
            out_specs=[IN_VMEM, IN_VMEM],
            scratch_shapes=[
                pltpu.VMEM(tile_values.shape, tile_values.dtype),
                pltpu.VMEM(basis.shape, basis.dtype),
                pltpu.VMEM((blocks, TILE, RANK), jnp.bfloat16),
                pltpu.SemaphoreType.DMA((tiles,)),
                pltpu.SemaphoreType.DMA,
            ],
        ),
        out_shape=[pltpu.VMEM(HALF, jnp.float32)] * 2,
        compiler_params=pltpu.CompilerParams(vmem_limit_bytes=16 << 20),
        name="local_product",
    )(left_out(tile_row), left_out(tile_col), core, left_out(tile_values), left_out(basis))


def sum_and_spread(parts, copies):
    total = jnp.sum(parts, axis=0)
    return jnp.broadcast_to(total, (copies,) + total.shape)


def gram_kernel(rows_ref, out_ref):
    rows = rows_ref[...]
    out_ref[...] = lax.dot_general(
        rows,
        rows,
        (((0,), (0,)), ((), ())),
        precision=HIGHEST,
        preferred_element_type=jnp.float32,
    )


def gram_terms(rows):
    return pl.pallas_call(
        gram_kernel,
        in_specs=[IN_VMEM],
        out_specs=IN_VMEM,
        out_shape=pltpu.VMEM((RANK, RANK), jnp.float32),
        compiler_params=pltpu.CompilerParams(vmem_limit_bytes=24 << 20),
        name="gram_terms",
    )(held(rows))


def lane(v, j):
    return jnp.broadcast_to(v[:, j : j + 1], (8, 128))


def sub(v, i):
    return jnp.broadcast_to(v[i : i + 1, :], v.shape)


def total(terms):
    while len(terms) > 1:
        terms = [x + y for x, y in zip(terms[::2], terms[1::2])] + terms[len(terms) & ~1 :]
    return terms[0]


def invert_factor(block, at):
    e = {}
    for i in range(8):
        row = sub(block, i)
        for j in range(i + 1):
            e[i, j] = lane(row, at + j)
    inv = {}
    for j in range(8):
        r = lax.rsqrt(e[j, j])
        inv[j, j] = r
        for i in range(j + 1, 8):
            e[i, j] = e[i, j] * r
        for k in range(j + 1, 8):
            for i in range(k, 8):
                e[i, k] = e[i, k] - e[i, j] * e[k, j]
        for k in range(j):
            inv[j, k] = -r * total([e[j, i] * inv[i, k] for i in range(k, j)])
    place = lax.broadcasted_iota(jnp.int32, (8, 128), 0)
    zero = jnp.zeros((8, 128), jnp.float32)
    lower, upper = [], []
    for j in range(8):
        down = across = zero
        for i in range(j, 8):
            down = jnp.where(place == i, inv[i, j], down)
        for i in range(j + 1):
            across = jnp.where(place == i, inv[j, i], across)
        lower.append(down)
        upper.append(across)
    return lower, upper, inv


def combine(columns, rows):
    return [total([columns[j] * sub(piece, j) for j in range(8)]) for piece in rows]


def eliminate(refs, first):
    for k in range(16):
        here = slice(first + 8 * k, first + 8 * k + 8)
        pieces = [ref[here, :] for ref in refs]
        lower, upper, inverse = invert_factor(pieces[0], 8 * k)
        scaled = combine(lower, pieces)
        for ref, piece in zip(refs[1:], scaled[1:]):
            ref[here, :] = piece
        if k == 15:
            break
        there = slice(first + 8 * (k + 1), first + 8 * (k + 2))
        old = [ref[there, :] for ref in refs]
        ms = [lane(old[0], 8 * k + j) for j in range(8)]
        factor = [total([ms[i] * inverse[j, i] for i in range(j + 1)]) for j in range(8)]
        for ref, piece, by in zip(refs, old, scaled):
            ref[there, :] = piece - total([factor[j] * sub(by, j) for j in range(8)])
        if k + 2 < 16:
            solved = combine(upper, scaled)
            there = slice(first + 8 * (k + 2), first + 128)
            left = refs[0][there, 8 * k : 8 * k + 8]
            for ref, piece in zip(refs, solved):
                ref[there, :] -= jnp.dot(left, piece, precision=HIGHEST, preferred_element_type=jnp.float32)


def finish_kernel(at_ref, gram_ref, other_ref, rows_ref, out_ref, left_ref, right_ref, y_ref):
    s = (gram_ref[...] + other_ref[...]) * (1.0 / COLS)
    left_ref[...] = s[:, 0:128]
    right_ref[...] = s[:, 128:256]
    zl, far = at_ref[0], at_ref[1]
    rows = jnp.concatenate(
        [
            rows_ref[zl * 4 + yl * 2 + xl, far + xh]
            for yl in range(2)
            for xh in range(2)
            for xl in range(2)
        ],
        axis=0,
    )
    y_ref[...] = jnp.concatenate([rows, jnp.zeros_like(rows)], axis=0).T
    eliminate((left_ref, right_ref, y_ref), 0)
    u, ua = right_ref[0:128, :], y_ref[0:128, :]
    for ref, by in ((right_ref, u), (y_ref, ua)):
        ref[128:256, :] -= lax.dot_general(
            u, by, (((0,), (0,)), ((), ())), precision=HIGHEST, preferred_element_type=jnp.float32
        )
    eliminate((right_ref, y_ref), 128)
    out_ref[...] = y_ref[...].T[0:64, :]


def finish(at, gram, other, rows):
    return pl.pallas_call(
        finish_kernel,
        in_specs=[pl.BlockSpec(memory_space=pltpu.SMEM), IN_VMEM, IN_VMEM, IN_VMEM],
        out_shape=jax.ShapeDtypeStruct((64, RANK), jnp.float32),
        scratch_shapes=[pltpu.VMEM((RANK, 128), jnp.float32)] * 3,
        compiler_params=pltpu.CompilerParams(vmem_limit_bytes=12 << 20),
        name="finish",
    )(at, held(gram), held(other), held(rows))


def members(axes):
    index = np.arange(512).reshape(SIZES)
    inner = [AXES.index(a) for a in axes]
    outer = [i for i in range(len(AXES)) if i not in inner]
    count = math.prod(SIZES[i] for i in inner)
    return index.transpose(outer + inner).reshape(-1, count).tolist()


def cubes():
    groups = []
    for core in range(2):
        for z, y, x in itertools.product(range(0, 8, 2), range(0, 8, 2), range(0, 4, 2)):
            group = [0] * 8
            for dz, dy, dx in itertools.product(range(2), repeat=3):
                at = ((z + core + dz) % 8, (y + core + dy) % 8, (x + core + dx) % 4)
                place = (at[0] % 2) * 4 + (at[1] % 2) * 2 + at[2] % 2
                group[place] = ((at[0] * 4 + at[1] // 2) * 2 + core) * 8 + (at[1] % 2) * 4 + at[2]
            groups.append(group)
    return groups


def exchange(x, groups):
    return lax.all_to_all(x, ALL, 0, 0, axis_index_groups=groups, tiled=True)


PARTNERS = [(i, i ^ 8) for i in range(512)]


def body(tile_values, tile_row, tile_col, basis):
    wide = lax.axis_index("wide").astype(jnp.int32)
    core, z, yh = wide & 1, wide >> 3, (wide >> 1) & 3
    near, far = cubes(), members(FAR)
    keep, send = local_product(tile_values, tile_row, tile_col, basis, core.reshape(1))
    both = keep + lax.ppermute(send, ALL, PARTNERS)
    over_near = jnp.sum(exchange(both, near), axis=0)
    far_rows = exchange(sum_and_spread(exchange(over_near, far), 32), far)
    rows = exchange(jnp.broadcast_to(far_rows, HALF), near)
    gram = gram_terms(rows.reshape(COLS // 2, RANK))
    other = lax.ppermute(gram, ALL, PARTNERS)
    at = jnp.stack([z & 1, (z >> 1) * 8 + yh * 2])
    return finish(at, gram, other, rows)


def solution(mesh):
    axes = mesh.axis_names
    in_specs = (P(axes, None, None), P(axes), P(axes), P(axes, None))
    return jax.shard_map(body, mesh=mesh, in_specs=in_specs, out_specs=P("wide", None), check_vma=False)
```

```python
import itertools
import math

import jax
import jax.numpy as jnp
import numpy as np
from jax import lax
from jax.experimental import pallas as pl
from jax.experimental.pallas import tpu as pltpu
from jax.sharding import PartitionSpec as P

AXES = ("zh", "zl", "yh", "core", "yl", "xh", "xl")
SIZES = (4, 2, 4, 2, 2, 2, 2)
ALL = ("wide", "narrow")
FAR = ("zh", "yh", "xh")
TILE = 512
RANK = 256
COLS = 4096
HIGHEST = lax.Precision.HIGHEST
HALF = (8, 32, 8, RANK)
IN_VMEM = pl.BlockSpec(memory_space=pltpu.VMEM)


def held(x):
    return pltpu.with_memory_space_constraint(x, pltpu.VMEM)


def left_out(x):
    return pltpu.with_memory_space_constraint(x, pltpu.HBM)


def product_kernel(row_ref, col_ref, core_ref, tile_ref, basis_ref, keep_ref, send_ref, tiles, rows, rounded, tile_sem, row_sem):
    count = tiles.shape[0]
    rows_in = pltpu.make_async_copy(basis_ref, rows, row_sem)
    rows_in.start()
    for t in range(count):
        pltpu.make_async_copy(tile_ref.at[t], tiles.at[t], tile_sem.at[t]).start()
    keep_ref[...] = jnp.zeros_like(keep_ref)
    send_ref[...] = jnp.zeros_like(send_ref)
    rows_in.wait()
    rounded[...] = rows[...].astype(jnp.bfloat16).reshape(rounded.shape)

    def step(t, carry):
        pltpu.make_async_copy(tile_ref.at[t], tiles.at[t], tile_sem.at[t]).wait()
        c = col_ref[t]
        near, far = (c & 1) * 4, (c >> 1) * 8
        res = lax.dot_general(
            tiles[t],
            rounded[row_ref[t]],
            (((0,), (0,)), ((), ())),
            preferred_element_type=jnp.float32,
        )

        def add(halves):
            for yh in range(4):
                for core in range(2):
                    for yl in range(2):
                        for xh in range(2):
                            for xl in range(2):
                                i = (((yh * 2 + core) * 2 + yl) * 2 + xh) * 2 + xl
                                halves[core][near + yl * 2 + xl, far + yh * 2 + xh] += res[8 * i : 8 * i + 8, :]

        @pl.when(core_ref[0] == 0)
        def _():
            add((keep_ref, send_ref))

        @pl.when(core_ref[0] == 1)
        def _():
            add((send_ref, keep_ref))

        return carry

    lax.fori_loop(0, count, step, 0)


def local_product(tile_values, tile_row, tile_col, basis, core):
    tiles = tile_values.shape[0]
    blocks = basis.shape[0] // TILE
    outside = pl.BlockSpec(memory_space=pltpu.HBM)
    return pl.pallas_call(
        product_kernel,
        grid_spec=pltpu.PrefetchScalarGridSpec(
            num_scalar_prefetch=3,
            grid=(),
            in_specs=[outside, outside],
            out_specs=[IN_VMEM, IN_VMEM],
            scratch_shapes=[
                pltpu.VMEM(tile_values.shape, tile_values.dtype),
                pltpu.VMEM(basis.shape, basis.dtype),
                pltpu.VMEM((blocks, TILE, RANK), jnp.bfloat16),
                pltpu.SemaphoreType.DMA((tiles,)),
                pltpu.SemaphoreType.DMA,
            ],
        ),
        out_shape=[pltpu.VMEM(HALF, jnp.float32)] * 2,
        compiler_params=pltpu.CompilerParams(vmem_limit_bytes=16 << 20),
        name="local_product",
    )(left_out(tile_row), left_out(tile_col), core, left_out(tile_values), left_out(basis))


def sum_and_spread(parts, copies):
    total = jnp.sum(parts, axis=0)
    return jnp.broadcast_to(total, (copies,) + total.shape)


def gram_kernel(rows_ref, out_ref):
    def inner(a, b):
        return lax.dot_general(
            a, b, (((0,), (0,)), ((), ())), precision=HIGHEST, preferred_element_type=jnp.float32
        )

    left, right = rows_ref[:, 0:128], rows_ref[:, 128:256]
    out_ref[0:128, :] = inner(left, rows_ref[...])
    out_ref[128:256, 0:128] = out_ref[0:128, 128:256].T
    out_ref[128:256, 128:256] = inner(right, right)


def gram_terms(rows):
    return pl.pallas_call(
        gram_kernel,
        in_specs=[IN_VMEM],
        out_specs=IN_VMEM,
        out_shape=pltpu.VMEM((RANK, RANK), jnp.float32),
        compiler_params=pltpu.CompilerParams(vmem_limit_bytes=24 << 20),
        name="gram_terms",
    )(held(rows))


def lane(v, j):
    return jnp.broadcast_to(v[:, j : j + 1], (8, 128))


def sub(v, i):
    return jnp.broadcast_to(v[i : i + 1, :], v.shape)


def total(terms):
    while len(terms) > 1:
        terms = [x + y for x, y in zip(terms[::2], terms[1::2])] + terms[len(terms) & ~1 :]
    return terms[0]


def invert_factor(block, at):
    e = {}
    for i in range(8):
        row = sub(block, i)
        for j in range(i + 1):
            e[i, j] = lane(row, at + j)
    inv = {}
    for j in range(8):
        r = lax.rsqrt(e[j, j])
        inv[j, j] = r
        for i in range(j + 1, 8):
            e[i, j] = e[i, j] * r
        for k in range(j + 1, 8):
            for i in range(k, 8):
                e[i, k] = e[i, k] - e[i, j] * e[k, j]
        for k in range(j):
            inv[j, k] = -r * total([e[j, i] * inv[i, k] for i in range(k, j)])
    place = lax.broadcasted_iota(jnp.int32, (8, 128), 0)
    zero = jnp.zeros((8, 128), jnp.float32)
    lower, upper = [], []
    for j in range(8):
        down = across = zero
        for i in range(j, 8):
            down = jnp.where(place == i, inv[i, j], down)
        for i in range(j + 1):
            across = jnp.where(place == i, inv[j, i], across)
        lower.append(down)
        upper.append(across)
    return lower, upper, inv


def combine(columns, rows):
    return [total([columns[j] * sub(piece, j) for j in range(8)]) for piece in rows]


def eliminate(refs, first):
    for k in range(16):
        here = slice(first + 8 * k, first + 8 * k + 8)
        pieces = [ref[here, :] for ref in refs]
        lower, upper, inverse = invert_factor(pieces[0], 8 * k)
        scaled = combine(lower, pieces)
        for ref, piece in zip(refs[1:], scaled[1:]):
            ref[here, :] = piece
        if k == 15:
            break
        there = slice(first + 8 * (k + 1), first + 8 * (k + 2))
        old = [ref[there, :] for ref in refs]
        ms = [lane(old[0], 8 * k + j) for j in range(8)]
        factor = [total([ms[i] * inverse[j, i] for i in range(j + 1)]) for j in range(8)]
        for ref, piece, by in zip(refs, old, scaled):
            ref[there, :] = piece - total([factor[j] * sub(by, j) for j in range(8)])
        if k + 2 < 16:
            solved = combine(upper, scaled)
            there = slice(first + 8 * (k + 2), first + 128)
            left = refs[0][there, 8 * k : 8 * k + 8]
            for ref, piece in zip(refs, solved):
                ref[there, :] -= jnp.dot(left, piece, precision=HIGHEST, preferred_element_type=jnp.float32)


def finish_kernel(at_ref, gram_ref, other_ref, rows_ref, out_ref, left_ref, right_ref, y_ref):
    s = (gram_ref[...] + other_ref[...]) * (1.0 / COLS)
    left_ref[...] = s[:, 0:128]
    right_ref[...] = s[:, 128:256]
    zl, far = at_ref[0], at_ref[1]
    rows = jnp.concatenate(
        [
            rows_ref[zl * 4 + yl * 2 + xl, far + xh]
            for yl in range(2)
            for xh in range(2)
            for xl in range(2)
        ],
        axis=0,
    )
    y_ref[...] = jnp.concatenate([rows, jnp.zeros_like(rows)], axis=0).T
    eliminate((left_ref, right_ref, y_ref), 0)
    u, ua = right_ref[0:128, :], y_ref[0:128, :]
    for ref, by in ((right_ref, u), (y_ref, ua)):
        ref[128:256, :] -= lax.dot_general(
            u, by, (((0,), (0,)), ((), ())), precision=HIGHEST, preferred_element_type=jnp.float32
        )
    eliminate((right_ref, y_ref), 128)
    out_ref[...] = y_ref[...].T[0:64, :]


def finish(at, gram, other, rows):
    return pl.pallas_call(
        finish_kernel,
        in_specs=[pl.BlockSpec(memory_space=pltpu.SMEM), IN_VMEM, IN_VMEM, IN_VMEM],
        out_shape=jax.ShapeDtypeStruct((64, RANK), jnp.float32),
        scratch_shapes=[pltpu.VMEM((RANK, 128), jnp.float32)] * 3,
        compiler_params=pltpu.CompilerParams(vmem_limit_bytes=12 << 20),
        name="finish",
    )(at, held(gram), held(other), held(rows))


def members(axes):
    index = np.arange(512).reshape(SIZES)
    inner = [AXES.index(a) for a in axes]
    outer = [i for i in range(len(AXES)) if i not in inner]
    count = math.prod(SIZES[i] for i in inner)
    return index.transpose(outer + inner).reshape(-1, count).tolist()


def cubes():
    groups = []
    for core in range(2):
        for z, y, x in itertools.product(range(0, 8, 2), range(0, 8, 2), range(0, 4, 2)):
            group = [0] * 8
            for dz, dy, dx in itertools.product(range(2), repeat=3):
                at = ((z + core + dz) % 8, (y + core + dy) % 8, (x + core + dx) % 4)
                place = (at[0] % 2) * 4 + (at[1] % 2) * 2 + at[2] % 2
                group[place] = ((at[0] * 4 + at[1] // 2) * 2 + core) * 8 + (at[1] % 2) * 4 + at[2]
            groups.append(group)
    return groups


def exchange(x, groups):
    return lax.all_to_all(x, ALL, 0, 0, axis_index_groups=groups, tiled=True)


PARTNERS = [(i, i ^ 8) for i in range(512)]


def body(tile_values, tile_row, tile_col, basis):
    wide = lax.axis_index("wide").astype(jnp.int32)
    core, z, yh = wide & 1, wide >> 3, (wide >> 1) & 3
    near, far = cubes(), members(FAR)
    keep, send = local_product(tile_values, tile_row, tile_col, basis, core.reshape(1))
    both = keep + lax.ppermute(send, ALL, PARTNERS)
    over_near = jnp.sum(exchange(both, near), axis=0)
    far_rows = exchange(sum_and_spread(exchange(over_near, far), 32), far)
    rows = exchange(jnp.broadcast_to(far_rows, HALF), near)
    gram = gram_terms(rows.reshape(COLS // 2, RANK))
    other = lax.ppermute(gram, ALL, PARTNERS)
    at = jnp.stack([z & 1, (z >> 1) * 8 + yh * 2])
    return finish(at, gram, other, rows)


def solution(mesh):
    axes = mesh.axis_names
    in_specs = (P(axes, None, None), P(axes), P(axes), P(axes, None))
    return jax.shard_map(body, mesh=mesh, in_specs=in_specs, out_specs=P("wide", None), check_vma=False)
```
